512 devices in a mesh: row: 32 (over z, x), rep: 8 (over y), feat: 2 (over core).
Axes of the slice: x: 4, y: 8, z: 8, core: 2. Of those that a mesh axis runs over, the one named last changes fastest.
Arguments:
- features: bfloat16 [32768, 256], P(('row', 'rep'), 'feat'), may hold values from -6 to 6
- weight: float32 [256, 256], replicated, may hold values from -0.375 to 0.375
- layer_bias: float32 [256], replicated, may hold values from -3 to 3
- cotangent: float32 [32768, 256], P(('row', 'rep'), 'feat'), may hold values from -6 to 6
- adj_tiles: bfloat16 [32, 8, 8, 8, 128, 128], P('row', 'rep', None, 'feat'), may hold values from -0.3125 to 0.3125
- tile_source: int32 [32, 8, 8, 8], P('row', 'rep', None, 'feat'), may hold values from 0 to 31
- tile_count: int32 [32, 8, 8], P('row', 'rep'), may hold values from 1 to 8, as said below
Outputs:
- output: float32 [32768, 256], P(('row', 'rep'), 'feat')
- grad_features: float32 [32768, 256], P(('row', 'rep'), 'feat')
- grad_weight: float32 [256, 256], P(None, 'feat')
- grad_bias: float32 [256], P('feat')
The draws below stay inside these ranges and needn't reach their ends.
Inputs may be any that keep to these rules, and one draw needn't show every extreme that they name: `tile_count`: each list has at least one live slot; some list in every draw has all 8 slots live.
All inputs are finite; a program needn't handle non-finite values.
Results may differ from the reference program's by a relative error of at most 0.0029.
Values may be sent and summed in bfloat16 or wider, within the bound.
No kernel may reach another device: no remote copies, remote signals or barrier semaphores. Data moves between devices by JAX's collectives and lax.ppermute only.
A program may use at most 64 MiB of HBM per device.

```python
import jax
import jax.numpy as jnp
from jax import lax

F = 256
BLOCK = 128
SLOTS = 8
NODES = 32768
N_ROW = 32
N_REP = 8


def draw_tile_count(key, part):
    folded = jax.random.fold_in(key, 7)
    key_left, key_right, key_full = jax.random.split(folded, 3)
    grid_shape = (N_ROW, N_REP, N_REP)
    draw_left = jax.random.randint(key_left, grid_shape, 1, SLOTS + 1)
    draw_right = jax.random.randint(key_right, grid_shape, 1, SLOTS + 1)
    counts = jnp.minimum(draw_left, draw_right).reshape(-1)
    where_full = jax.random.randint(key_full, (), 0, N_ROW * N_REP * N_REP)
    counts = jnp.where(jnp.arange(N_ROW * N_REP * N_REP) == where_full, SLOTS, counts)
    return counts.reshape(grid_shape).astype(jnp.int32)


def place_ends(result, own_key, least, high):
    longest = result.shape.index(max(result.shape))
    spots = []
    for shift in (0, 1):
        where = [jax.random.randint(jax.random.fold_in(own_key, axis), (), 0, length) for axis, length in enumerate(result.shape)]
        where[longest] = (where[longest] + shift) % result.shape[longest]
        spots.append(tuple(where))
    return result.at[spots[0]].set(least).at[spots[1]].set(high)


def levels(rng, dims, shards, low, largest):
    def one(position, shards_of):
        heights = jax.random.uniform(jax.random.fold_in(jax.random.fold_in(rng, 6), position), (shards_of,), jnp.float32, low / len(shards), largest / len(shards))
        return jnp.repeat(jnp.exp(heights), dims[position] // shards_of).reshape((-1,) + (1,) * (len(dims) - position - 1))

    gain = one(*shards[0])
    for cut in shards[1:]:
        gain = gain * one(*cut)
    return gain


def gaussian(rng, dims, scale, limit, shards=(), held_as=jnp.bfloat16):
    array = jax.random.normal(rng, dims, jnp.float32) * scale
    if len(shards) > 0:
        array = levels(rng, dims, shards, -0.22, 0.18) * array
    return jnp.clip(array, min=-limit, max=limit).astype(held_as)


def setup_inputs(seed: int = 0) -> dict:
    key_list = jax.random.split(jax.random.key(seed), 8)
    features = gaussian(key_list[0], (NODES, F), 1.0, 6.0, ((0, 256), (1, 2)))
    weight = gaussian(key_list[1], (F, F), F ** -0.5, 0.375, (), jnp.float32)
    layer_bias = gaussian(key_list[2], (F,), 0.5, 3.0, (), jnp.float32)
    cotangent = gaussian(key_list[3], (NODES, F), 1.0, 6.0, ((0, 256), (1, 2)), jnp.float32)
    adj_tiles = gaussian(key_list[4], (N_ROW, N_REP, N_REP, SLOTS, BLOCK, BLOCK), (BLOCK * SLOTS // 3) ** -0.5, 0.3125, ((0, 32), (1, 8), (3, 2)))
    tile_source = place_ends(jax.random.randint(key_list[5], (N_ROW, N_REP, N_REP, SLOTS), 0, N_ROW), jax.random.fold_in(key_list[5], 1), 0, N_ROW - 1).astype(jnp.int32)
    tile_count = draw_tile_count(jax.random.fold_in(key_list[7], 71), 0)
    return {"features": features, "weight": weight, "layer_bias": layer_bias, "cotangent": cotangent, "adj_tiles": adj_tiles, "tile_source": tile_source, "tile_count": tile_count}


def reference(features, weight, layer_bias, cotangent, adj_tiles, tile_source, tile_count):
    rows_count, reps_count, dests_count, slots_count = tile_source.shape
    width = features.shape[1]
    highest = lax.Precision.HIGHEST
    feat_blocks = features.reshape(rows_count, reps_count, BLOCK, width)
    live_mask = jnp.arange(slots_count, dtype=jnp.int32)[None, None, None, :] < tile_count[..., None]

    def group_sum(row_index):
        def add_class(running, class_index):
            tile_set = adj_tiles[row_index, class_index]
            keep_mask = live_mask[row_index, class_index]
            masked = jnp.where(keep_mask[:, :, None, None], tile_set, jnp.zeros_like(tile_set)).astype(jnp.float32)
            source_ids = tile_source[row_index, class_index]
            chosen = feat_blocks[source_ids, class_index].astype(jnp.float32)
            return running + jnp.einsum('dkij,dkjc->dic', masked, chosen, precision=highest), None
        start_zero = jnp.zeros((dests_count, BLOCK, width), jnp.float32)
        summed, unused = lax.scan(add_class, start_zero, jnp.arange(reps_count, dtype=jnp.int32))
        return summed

    aggregate_all = lax.map(group_sum, jnp.arange(rows_count, dtype=jnp.int32))
    aggregate_flat = aggregate_all.reshape(-1, width)
    preact = jnp.dot(aggregate_flat, weight, precision=highest) + layer_bias
    sigmoid_val = jax.nn.sigmoid(preact)
    output = preact * sigmoid_val
    grad_preact = cotangent * (sigmoid_val * (1.0 + preact * (1.0 - sigmoid_val)))
    grad_weight = jnp.dot(aggregate_flat.T, grad_preact, precision=highest)
    grad_bias = jnp.sum(grad_preact, axis=0)
    grad_aggregate = jnp.dot(grad_preact, weight.T, precision=highest).astype(jnp.bfloat16)
    grad_blocks = grad_aggregate.reshape(rows_count, dests_count, BLOCK, width)

    def add_pair(accumulated, pair_index):
        row_index = pair_index // reps_count
        class_index = pair_index % reps_count
        tile_set = adj_tiles[row_index, class_index]
        keep_mask = live_mask[row_index, class_index]
        masked = jnp.where(keep_mask[:, :, None, None], tile_set, jnp.zeros_like(tile_set)).astype(jnp.float32)
        grad_rows = grad_blocks[row_index].astype(jnp.float32)
        contrib = jnp.einsum('dkij,dic->dkjc', masked, grad_rows, precision=highest)
        source_ids = tile_source[row_index, class_index]
        onehot = (source_ids[:, :, None] == jnp.arange(rows_count, dtype=jnp.int32)[None, None, :]).astype(jnp.float32)
        addend = jnp.einsum('dks,dkjc->sjc', onehot, contrib, precision=highest)
        previous = lax.dynamic_index_in_dim(accumulated, class_index, 1, keepdims=False)
        return lax.dynamic_update_index_in_dim(accumulated, previous + addend, class_index, 1), None

    start_grad = jnp.zeros((rows_count, reps_count, BLOCK, width), jnp.float32)
    grad_all, unused = lax.scan(add_pair, start_grad, jnp.arange(rows_count * reps_count, dtype=jnp.int32))
    return output, grad_all.reshape(-1, width), grad_weight, grad_bias
```

```python
import jax
import jax.numpy as jnp
from jax import lax
from jax.experimental import pallas as pl
from jax.experimental.pallas import tpu as pltpu
from jax.sharding import PartitionSpec as P

BF = jnp.bfloat16
F32 = jnp.float32
HI = lax.Precision.HIGHEST
VM = pl.BlockSpec(memory_space=pltpu.VMEM)
SM = pl.BlockSpec(memory_space=pltpu.SMEM)


def slot_lists(own_ref, peer_ref, feat):
    return ((own_ref, feat), (peer_ref, 1 - feat))


def forward_kernel(count_ref, source_ref, own_ref, peer_ref, panel_ref, out_ref):
    feat = lax.axis_index("feat")
    dests, half = own_ref.shape[:2]
    for d in range(dests):
        lefts, rights = [], []
        for tiles_ref, side in slot_lists(own_ref, peer_ref, feat):
            for j in range(half):
                block = panel_ref[source_ref[side, d, j]]
                live = side * half + j < count_ref[d]
                lefts.append(tiles_ref[d, j])
                rights.append(jnp.where(live, block, jnp.zeros_like(block)))
        out_ref[d] = jnp.dot(
            jnp.concatenate(lefts, axis=1),
            jnp.concatenate(rights, axis=0),
            preferred_element_type=F32,
        )


def collect_kernel(parts_ref, cotangent_ref, out_ref):
    rows = cotangent_ref.shape[0]
    total = parts_ref[0]
    for p in range(1, parts_ref.shape[0]):
        total = total + parts_ref[p]
    out_ref[:rows] = total
    out_ref[rows:] = cotangent_ref[...]


def node_kernel(both_ref, weight_ref, bias_ref, out_ref, pay_ref):
    first = lax.axis_index("feat") == 0
    rows, cols = out_ref.shape
    reps = pay_ref.shape[0]
    aggregate = jnp.concatenate([both_ref[:rows], both_ref[2 * rows : 3 * rows]], axis=1)
    cotangent = jnp.concatenate([both_ref[rows : 2 * rows], both_ref[3 * rows :]], axis=1)
    preact = jnp.dot(aggregate, weight_ref[...], precision=HI, preferred_element_type=F32) + bias_ref[...]
    sig = jax.nn.sigmoid(preact)
    output = preact * sig
    slope = cotangent * (sig * (1.0 + preact * (1.0 - sig)))
    out_ref[...] = jnp.where(first, output[:, :cols], output[:, cols:])
    slope_own = jnp.where(first, slope[:, :cols], slope[:, cols:])
    weight_rows = jnp.where(first, weight_ref[:cols], weight_ref[cols:])
    grad_t = lax.dot_general(
        weight_rows, slope, (((1,), (1,)), ((), ())), precision=HI, preferred_element_type=F32
    ).astype(BF)
    weight_term = lax.dot_general(
        aggregate, slope_own, (((0,), (0,)), ((), ())), precision=HI, preferred_element_type=F32
    )
    bias_term = jnp.sum(slope_own, axis=0, keepdims=True)
    chunk = weight_term.shape[0] // reps
    pad = jnp.where(lax.broadcasted_iota(jnp.int32, (8, cols), 0) == 0, bias_term, 0.0)
    for q in range(reps):
        piece = jnp.concatenate([weight_term[q * chunk : (q + 1) * chunk], pad], axis=0)
        upper = piece.astype(BF)
        lower = (piece - upper.astype(F32)).astype(BF)
        pay_ref[q, :rows] = grad_t
        pay_ref[q, rows : rows + chunk + 8] = upper
        pay_ref[q, rows + chunk + 8 :] = lower


def backward_kernel(count_ref, source_ref, own_ref, peer_ref, pay_ref, out_ref, total_ref, terms_ref):
    feat = lax.axis_index("feat")
    dests, half, rows = own_ref.shape[:3]
    extra = out_ref.shape[1] - rows
    total_ref[...] = jnp.zeros_like(total_ref)
    for d in range(dests):
        grad_t = pay_ref[d, :rows]
        for h, (tiles_ref, side) in enumerate(slot_lists(own_ref, peer_ref, feat)):
            product = jnp.dot(
                grad_t,
                jnp.concatenate([tiles_ref[d, j] for j in range(half)], axis=1),
                preferred_element_type=F32,
            )
            for j in range(half):
                terms_ref[(d * 2 + h) * half + j] = product[:, j * rows : (j + 1) * rows]
    for d in range(dests):
        for h, (tiles_ref, side) in enumerate(slot_lists(own_ref, peer_ref, feat)):
            for j in range(half):

                @pl.when(side * half + j < count_ref[d])
                def _(d=d, h=h, j=j, side=side):
                    source = source_ref[side, d, j]
                    total_ref[source] = total_ref[source] + terms_ref[(d * 2 + h) * half + j]

    piece = jnp.zeros((extra, rows), F32)
    for q in range(pay_ref.shape[0]):
        piece = piece + pay_ref[q, rows : rows + extra].astype(F32) + pay_ref[q, rows + extra :].astype(F32)
    piece = piece.astype(BF)
    for s in range(out_ref.shape[0]):
        out_ref[s, :rows] = total_ref[s].astype(BF)
        out_ref[s, rows:] = piece


def finish_kernel(parts_ref, grad_ref, piece_ref):
    rows = grad_ref.shape[0]
    total = parts_ref[0].astype(F32)
    for s in range(1, parts_ref.shape[0]):
        total = total + parts_ref[s].astype(F32)
    grad_ref[...] = total[:rows].T
    for q in range(piece_ref.shape[0]):
        piece_ref[q] = total[rows:]


def shape(dims, dtype):
    return jax.ShapeDtypeStruct(dims, dtype)


def local(features, weight, layer_bias, cotangent, adj_tiles, tile_source, tile_count):
    rows, cols = features.shape
    n_row = lax.axis_size("row")
    own = adj_tiles[0, 0]
    counts = tile_count[0, 0]
    dests, half = own.shape[:2]
    reps = lax.axis_size("rep")
    width = weight.shape[0]
    extra = width // reps + 8
    peer = lax.ppermute(own, "feat", [(0, 1), (1, 0)])
    sources = lax.all_gather(tile_source[0, 0], "feat")
    panel = lax.all_to_all(jnp.broadcast_to(features[None], (n_row, rows, cols)), "row", 0, 0, tiled=True)
    partial = pl.pallas_call(
        forward_kernel,
        out_shape=shape((dests, rows, cols), F32),
        in_specs=[SM, SM, VM, VM, VM],
        out_specs=VM,
    )(counts, sources, own, peer, panel)
    parts = lax.all_to_all(partial, "rep", 0, 0, tiled=True)
    stacked = pl.pallas_call(
        collect_kernel, out_shape=shape((2 * rows, cols), F32), in_specs=[VM, VM], out_specs=VM
    )(parts, cotangent)
    both = lax.all_gather(stacked, "feat", axis=0, tiled=True)
    output, pay = pl.pallas_call(
        node_kernel,
        out_shape=(shape((rows, cols), F32), shape((reps, rows + 2 * extra, cols), BF)),
        in_specs=[VM, VM, VM],
        out_specs=(VM, VM),
    )(both, weight, layer_bias[None])
    pay = lax.all_to_all(pay, "rep", 0, 0, tiled=True)
    sends = pl.pallas_call(
        backward_kernel,
        out_shape=shape((n_row, rows + extra, cols), BF),
        in_specs=[SM, SM, VM, VM, VM],
        out_specs=VM,
        scratch_shapes=[
            pltpu.VMEM((n_row, cols, rows), F32),
            pltpu.VMEM((dests * 2 * half, cols, rows), F32),
        ],
    )(counts, sources, own, peer, pay)
    arrived = lax.all_to_all(sends, "row", 0, 0, tiled=True)
    grad_features, pieces = pl.pallas_call(
        finish_kernel,
        out_shape=(shape((rows, cols), F32), shape((reps, extra, cols), F32)),
        in_specs=[VM],
        out_specs=(VM, VM),
    )(arrived)
    pieces = lax.all_to_all(pieces, "rep", 0, 0, tiled=True)
    grad_weight = pieces[:, : extra - 8].reshape(width, cols)
    grad_bias = pieces[0, extra - 8]
    return output, grad_features, grad_weight, grad_bias


def solution(mesh):
    in_specs = (
        P(("row", "rep"), "feat"),
        P(),
        P(),
        P(("row", "rep"), "feat"),
        P("row", "rep", None, "feat", None, None),
        P("row", "rep", None, "feat"),
        P("row", "rep", None),
    )
    out_specs = (P(("row", "rep"), "feat"), P(("row", "rep"), "feat"), P(None, "feat"), P("feat"))
    return jax.shard_map(local, mesh=mesh, in_specs=in_specs, out_specs=out_specs, check_vma=False)
```

```python
import jax
import jax.numpy as jnp
from jax import lax
from jax.experimental import pallas as pl
from jax.experimental.pallas import tpu as pltpu
from jax.sharding import Mesh, PartitionSpec as P

BF = jnp.bfloat16
F32 = jnp.float32
HI = lax.Precision.HIGHEST
VM = pl.BlockSpec(memory_space=pltpu.VMEM)
SM = pl.BlockSpec(memory_space=pltpu.SMEM)
ROOM = pltpu.CompilerParams(vmem_limit_bytes=24 << 20)


def slot_lists(own_ref, peer_ref, feat):
    return ((own_ref, feat), (peer_ref, 1 - feat))


def forward_kernel(count_ref, source_ref, own_ref, peer_ref, panel_ref, out_ref):
    feat = lax.axis_index("feat")
    dests, half = own_ref.shape[:2]
    for d in range(dests):
        lefts, rights = [], []
        for tiles_ref, side in slot_lists(own_ref, peer_ref, feat):
            for j in range(half):
                block = panel_ref[source_ref[side, d, j]]
                live = side * half + j < count_ref[d]
                lefts.append(tiles_ref[d, j])
                rights.append(jnp.where(live, block, jnp.zeros_like(block)))
        out_ref[d] = jnp.dot(
            jnp.concatenate(lefts, axis=1),
            jnp.concatenate(rights, axis=0),
            preferred_element_type=F32,
        )


def collect_kernel(parts_ref, out_ref):
    total = parts_ref[0]
    for p in range(1, parts_ref.shape[0]):
        total = total + parts_ref[p]
    out_ref[...] = total


def padded(bias_term):
    upper = bias_term.astype(BF).astype(F32)
    place = lax.broadcasted_iota(jnp.int32, (8, bias_term.shape[1]), 0)
    return jnp.where(place == 0, upper, jnp.where(place == 1, bias_term - upper, 0.0))


def folded(pad):
    return pad[0:1] + pad[1:2]


def node_kernel(aggregate_ref, cotangent_ref, weight_ref, bias_ref, out_ref, pay_ref):
    first = lax.axis_index("feat") == 0
    rows, cols = out_ref.shape
    reps = pay_ref.shape[0]
    aggregate = jnp.concatenate([aggregate_ref[:rows], aggregate_ref[rows:]], axis=1)
    cotangent = jnp.concatenate([cotangent_ref[:rows], cotangent_ref[rows:]], axis=1)
    preact = jnp.dot(aggregate, weight_ref[...], precision=HI, preferred_element_type=F32) + bias_ref[...]
    sig = jax.nn.sigmoid(preact)
    output = preact * sig
    slope = cotangent * (sig * (1.0 + preact * (1.0 - sig)))
    out_ref[...] = jnp.where(first, output[:, :cols], output[:, cols:])
    slope_own = jnp.where(first, slope[:, :cols], slope[:, cols:])
    weight_rows = jnp.where(first, weight_ref[:cols], weight_ref[cols:])
    grad_t = lax.dot_general(
        weight_rows, slope, (((1,), (1,)), ((), ())), precision=HI, preferred_element_type=F32
    ).astype(BF)
    weight_term = lax.dot_general(
        aggregate, slope_own, (((0,), (0,)), ((), ())), precision=HI, preferred_element_type=F32
    )
    pad = padded(jnp.sum(slope_own, axis=0, keepdims=True)).astype(BF)
    chunk = weight_term.shape[0] // reps
    for q in range(reps):
        pay_ref[q, :rows] = grad_t
        pay_ref[q, rows : rows + chunk] = weight_term[q * chunk : (q + 1) * chunk].astype(BF)
        pay_ref[q, rows + chunk :] = pad


def backward_kernel(count_ref, source_ref, own_ref, peer_ref, pay_ref, out_ref, total_ref, terms_ref):
    feat = lax.axis_index("feat")
    dests, half, rows = own_ref.shape[:3]
    groups = total_ref.shape[0]
    x_count = out_ref.shape[0]
    z_count = groups // x_count
    extra = pay_ref.shape[1] - rows
    total_ref[...] = jnp.zeros_like(total_ref)
    for d in range(dests):
        grad_t = pay_ref[d, :rows]
        for h, (tiles_ref, side) in enumerate(slot_lists(own_ref, peer_ref, feat)):
            product = jnp.dot(
                grad_t,
                jnp.concatenate([tiles_ref[d, j] for j in range(half)], axis=1),
                preferred_element_type=F32,
            )
            for j in range(half):
                terms_ref[(d * 2 + h) * half + j] = product[:, j * rows : (j + 1) * rows]
    for d in range(dests):
        for h, (tiles_ref, side) in enumerate(slot_lists(own_ref, peer_ref, feat)):
            for j in range(half):

                @pl.when(side * half + j < count_ref[d])
                def _(d=d, h=h, j=j, side=side):
                    source = source_ref[side, d, j]
                    total_ref[source] = total_ref[source] + terms_ref[(d * 2 + h) * half + j]

    piece = jnp.zeros((extra, rows), F32)
    for q in range(pay_ref.shape[0]):
        piece = piece + pay_ref[q, rows:].astype(F32)
    term = piece[: extra - 8]
    upper = term.astype(BF)
    lower = (term - upper.astype(F32)).astype(BF)
    pad = padded(folded(piece[extra - 8 :])).astype(BF)
    base = z_count * rows
    for x in range(x_count):
        for z in range(z_count):
            out_ref[x, z * rows : (z + 1) * rows] = total_ref[z * x_count + x].astype(BF)
        out_ref[x, base : base + extra - 8] = upper
        out_ref[x, base + extra - 8 : base + 2 * extra - 16] = lower
        out_ref[x, base + 2 * extra - 16 :] = pad


def middle_kernel(parts_ref, out_ref):
    z_count, high = out_ref.shape[:2]
    rows = parts_ref.shape[2]
    base = z_count * rows
    chunk = high - rows - 8

    def summed(start, size):
        total = parts_ref[0, start : start + size].astype(F32)
        for x in range(1, parts_ref.shape[0]):
            total = total + parts_ref[x, start : start + size].astype(F32)
        return total

    term = (summed(base, chunk) + summed(base + chunk, chunk)).astype(BF)
    pad = padded(folded(summed(base + 2 * chunk, 8))).astype(BF)
    for z in range(z_count):
        out_ref[z, :rows] = summed(z * rows, rows).astype(BF)
        out_ref[z, rows : rows + chunk] = term
        out_ref[z, rows + chunk :] = pad


def finish_kernel(parts_ref, grad_ref, bias_ref, piece_ref):
    rows = grad_ref.shape[0]
    chunk = piece_ref.shape[1]
    total = parts_ref[0].astype(F32)
    for s in range(1, parts_ref.shape[0]):
        total = total + parts_ref[s].astype(F32)
    grad_ref[...] = total[:rows].T
    bias_ref[...] = folded(total[rows + chunk :])
    for q in range(piece_ref.shape[0]):
        piece_ref[q] = total[rows : rows + chunk]


def shape(dims, dtype):
    return jax.ShapeDtypeStruct(dims, dtype)


def near(dims, dtype):
    return pltpu.VMEM(dims, dtype)


def held(array):
    return pltpu.with_memory_space_constraint(array, pltpu.VMEM)


def swap(array, axis):
    return held(lax.all_to_all(array, axis, 0, 0, tiled=True))


def local(features, weight, layer_bias, cotangent, adj_tiles, tile_source, tile_count):
    rows, cols = features.shape
    z_count, x_count = lax.axis_size("z"), lax.axis_size("x")
    n_row = z_count * x_count
    counts = tile_count[0, 0]
    dests, half = adj_tiles.shape[2:4]
    reps = lax.axis_size("rep")
    width = weight.shape[0]
    chunk = width // reps
    peer = held(lax.ppermute(adj_tiles[0, 0], "feat", [(0, 1), (1, 0)]))
    own = held(adj_tiles[0, 0])
    sources = lax.all_gather(tile_source[0, 0], "feat")
    cotangents = held(lax.all_gather(cotangent, "feat", axis=0, tiled=True))
    panel = swap(jnp.broadcast_to(features[None], (n_row, rows, cols)), ("z", "x"))
    partial = pl.pallas_call(
        forward_kernel,
        out_shape=near((dests, rows, cols), F32),
        in_specs=[SM, SM, VM, VM, VM],
        out_specs=VM,
        compiler_params=ROOM,
    )(counts, sources, own, peer, panel)
    own_aggregate = pl.pallas_call(
        collect_kernel,
        out_shape=near((rows, cols), F32),
        in_specs=[VM],
        out_specs=VM,
        compiler_params=ROOM,
    )(swap(partial, "rep"))
    aggregate = held(lax.all_gather(own_aggregate, "feat", axis=0, tiled=True))
    output, pay = pl.pallas_call(
        node_kernel,
        out_shape=(shape((rows, cols), F32), near((reps, rows + chunk + 8, cols), BF)),
        in_specs=[VM, VM, VM, VM],
        out_specs=(VM, VM),
        compiler_params=ROOM,
    )(aggregate, cotangents, held(weight), layer_bias[None])
    sends = pl.pallas_call(
        backward_kernel,
        out_shape=near((x_count, z_count * rows + 2 * chunk + 8, cols), BF),
        in_specs=[SM, SM, VM, VM, VM],
        out_specs=VM,
        compiler_params=ROOM,
        scratch_shapes=[
            pltpu.VMEM((n_row, cols, rows), F32),
            pltpu.VMEM((dests * 2 * half, cols, rows), F32),
        ],
    )(counts, sources, own, peer, swap(pay, "rep"))
    onward = pl.pallas_call(
        middle_kernel,
        out_shape=near((z_count, rows + chunk + 8, cols), BF),
        in_specs=[VM],
        out_specs=VM,
        compiler_params=ROOM,
    )(swap(sends, "x"))
    grad_features, grad_bias, pieces = pl.pallas_call(
        finish_kernel,
        out_shape=(shape((rows, cols), F32), shape((1, cols), F32), near((reps, chunk, cols), F32)),
        in_specs=[VM],
        out_specs=(VM, VM, VM),
        compiler_params=ROOM,
    )(swap(onward, "z"))
    grad_weight = lax.all_to_all(pieces, "rep", 0, 0, tiled=True).reshape(width, cols)
    return output, grad_features, grad_weight, grad_bias[0]


def solution(mesh):
    n_row, n_rep, n_feat = mesh.devices.shape
    x_count = 4 if n_row > 4 else 2
    fine = Mesh(mesh.devices.reshape(n_row // x_count, x_count, n_rep, n_feat), ("z", "x", "rep", "feat"))
    nodes = P(("z", "x", "rep"), "feat")
    in_specs = (
        nodes,
        P(),
        P(),
        nodes,
        P(("z", "x"), "rep", None, "feat", None, None),
        P(("z", "x"), "rep", None, "feat"),
        P(("z", "x"), "rep", None),
    )
    out_specs = (nodes, nodes, P(None, "feat"), P("feat"))
    return jax.shard_map(local, mesh=fine, in_specs=in_specs, out_specs=out_specs, check_vma=False)
```

```python
import jax
import jax.numpy as jnp
from jax import lax
from jax.experimental import pallas as pl
from jax.experimental.pallas import tpu as pltpu
from jax.sharding import Mesh, PartitionSpec as P

BF = jnp.bfloat16
F32 = jnp.float32
HI = lax.Precision.HIGHEST
VM = pl.BlockSpec(memory_space=pltpu.VMEM)
SM = pl.BlockSpec(memory_space=pltpu.SMEM)
ROOM = pltpu.CompilerParams(vmem_limit_bytes=24 << 20)


def slot_lists(own_ref, peer_ref, feat):
    return ((own_ref, feat), (peer_ref, 1 - feat))


def forward_kernel(count_ref, source_ref, own_ref, peer_ref, panel_ref, out_ref):
    feat = lax.axis_index("feat")
    dests, half = own_ref.shape[:2]
    for d in range(dests):
        lefts, rights = [], []
        for tiles_ref, side in slot_lists(own_ref, peer_ref, feat):
            for j in range(half):
                block = panel_ref[source_ref[side, d, j]]
                live = side * half + j < count_ref[d]
                lefts.append(tiles_ref[d, j])
                rights.append(jnp.where(live, block, jnp.zeros_like(block)))
        out_ref[d] = jnp.dot(
            jnp.concatenate(lefts, axis=1),
            jnp.concatenate(rights, axis=0),
            preferred_element_type=F32,
        )


def collect_kernel(parts_ref, out_ref):
    total = parts_ref[0]
    for p in range(1, parts_ref.shape[0]):
        total = total + parts_ref[p]
    out_ref[...] = total


def padded(bias_term):
    upper = bias_term.astype(BF).astype(F32)
    place = lax.broadcasted_iota(jnp.int32, (8, bias_term.shape[1]), 0)
    return jnp.where(place == 0, upper, jnp.where(place == 1, bias_term - upper, 0.0))


def folded(pad):
    return pad[0:1] + pad[1:2]


def node_kernel(aggregate_ref, cotangent_ref, weight_ref, bias_ref, out_ref, pay_ref):
    first = lax.axis_index("feat") == 0
    rows, cols = out_ref.shape
    reps = pay_ref.shape[0]
    aggregate = jnp.concatenate([aggregate_ref[:rows], aggregate_ref[rows:]], axis=1)
    cotangent = jnp.concatenate([cotangent_ref[:rows], cotangent_ref[rows:]], axis=1)
    preact = jnp.dot(aggregate, weight_ref[...], precision=HI, preferred_element_type=F32) + bias_ref[...]
    sig = jax.nn.sigmoid(preact)
    output = preact * sig
    slope = cotangent * (sig * (1.0 + preact * (1.0 - sig)))
    out_ref[...] = jnp.where(first, output[:, :cols], output[:, cols:])
    slope_own = jnp.where(first, slope[:, :cols], slope[:, cols:])
    weight_rows = jnp.where(first, weight_ref[:cols], weight_ref[cols:])
    grad_t = lax.dot_general(
        weight_rows, slope, (((1,), (1,)), ((), ())), precision=HI, preferred_element_type=F32
    ).astype(BF)
    weight_term = lax.dot_general(
        aggregate, slope_own, (((0,), (0,)), ((), ())), precision=HI, preferred_element_type=F32
    )
    pad = padded(jnp.sum(slope_own, axis=0, keepdims=True)).astype(BF)
    chunk = weight_term.shape[0] // reps
    for q in range(reps):
        pay_ref[q, :rows] = grad_t
        pay_ref[q, rows : rows + chunk] = weight_term[q * chunk : (q + 1) * chunk].astype(BF)
        pay_ref[q, rows + chunk :] = pad


def backward_kernel(count_ref, source_ref, own_ref, peer_ref, pay_ref, out_ref, total_ref, terms_ref):
    feat = lax.axis_index("feat")
    dests, half, rows = own_ref.shape[:3]
    groups = total_ref.shape[0]
    x_count = out_ref.shape[0]
    z_count = groups // x_count
    extra = pay_ref.shape[1] - rows
    total_ref[...] = jnp.zeros_like(total_ref)
    for d in range(dests):
        grad_t = pay_ref[d, :rows]
        for h, (tiles_ref, side) in enumerate(slot_lists(own_ref, peer_ref, feat)):
            product = jnp.dot(
                grad_t,
                jnp.concatenate([tiles_ref[d, j] for j in range(half)], axis=1),
                preferred_element_type=F32,
            )
            for j in range(half):
                terms_ref[(d * 2 + h) * half + j] = product[:, j * rows : (j + 1) * rows]
    for d in range(dests):
        for h, (tiles_ref, side) in enumerate(slot_lists(own_ref, peer_ref, feat)):
            for j in range(half):

                @pl.when(side * half + j < count_ref[d])
                def _(d=d, h=h, j=j, side=side):
                    source = source_ref[side, d, j]
                    total_ref[source] = total_ref[source] + terms_ref[(d * 2 + h) * half + j]

    piece = jnp.zeros((extra, rows), F32)
    for q in range(pay_ref.shape[0]):
        piece = piece + pay_ref[q, rows:].astype(F32)
    term = piece[: extra - 8]
    upper = term.astype(BF)
    lower = (term - upper.astype(F32)).astype(BF)
    pad = padded(folded(piece[extra - 8 :])).astype(BF)
    base = z_count * rows
    for x in range(x_count):
        for z in range(z_count):
            out_ref[x, z * rows : (z + 1) * rows] = total_ref[z * x_count + x].astype(BF)
        out_ref[x, base : base + extra - 8] = upper
        out_ref[x, base + extra - 8 : base + 2 * extra - 16] = lower
        out_ref[x, base + 2 * extra - 16 :] = pad


def middle_kernel(parts_ref, out_ref):
    z_count, high = out_ref.shape[:2]
    rows = parts_ref.shape[2]
    base = z_count * rows
    chunk = high - rows - 8

    def summed(start, size):
        total = parts_ref[0, start : start + size].astype(F32)
        for x in range(1, parts_ref.shape[0]):
            total = total + parts_ref[x, start : start + size].astype(F32)
        return total

    term = (summed(base, chunk) + summed(base + chunk, chunk)).astype(BF)
    pad = padded(folded(summed(base + 2 * chunk, 8))).astype(BF)
    for z in range(z_count):
        out_ref[z, :rows] = summed(z * rows, rows).astype(BF)
        out_ref[z, rows : rows + chunk] = term
        out_ref[z, rows + chunk :] = pad


def finish_kernel(parts_ref, grad_ref, bias_ref, piece_ref):
    rows = grad_ref.shape[0]
    chunk = piece_ref.shape[1]
    total = parts_ref[0].astype(F32)
    for s in range(1, parts_ref.shape[0]):
        total = total + parts_ref[s].astype(F32)
    grad_ref[...] = total[:rows].T
    bias_ref[...] = folded(total[rows + chunk :])
    for q in range(piece_ref.shape[0]):
        piece_ref[q] = total[rows : rows + chunk]


def shape(dims, dtype):
    return jax.ShapeDtypeStruct(dims, dtype)


def near(dims, dtype):
    return pltpu.VMEM(dims, dtype)


def held(array):
    return pltpu.with_memory_space_constraint(array, pltpu.VMEM)


def swap(array, axis):
    return held(lax.all_to_all(array, axis, 0, 0, tiled=True))


def local(features, weight, layer_bias, cotangent, adj_tiles, tile_source, tile_count):
    rows, cols = features.shape
    z_count, x_count = lax.axis_size("z"), lax.axis_size("x")
    n_row = z_count * x_count
    counts = tile_count[0, 0]
    dests, half = adj_tiles.shape[2:4]
    reps = lax.axis_size("rep")
    width = weight.shape[0]
    chunk = width // reps
    peer = held(lax.ppermute(adj_tiles[0, 0], "feat", [(0, 1), (1, 0)]))
    own = held(adj_tiles[0, 0])
    sources = lax.all_gather(tile_source[0, 0], "feat")
    cotangents = held(lax.all_gather(cotangent, "feat", axis=0, tiled=True))
    panel = swap(jnp.broadcast_to(features[None], (n_row, rows, cols)), ("z", "x"))
    panel, cotangents, near_weight, near_bias = lax.optimization_barrier(
        (panel, cotangents, held(weight), held(layer_bias[None]))
    )
    partial = pl.pallas_call(
        forward_kernel,
        out_shape=near((dests, rows, cols), F32),
        in_specs=[SM, SM, VM, VM, VM],
        out_specs=VM,
        compiler_params=ROOM,
    )(counts, sources, own, peer, panel)
    own_aggregate = pl.pallas_call(
        collect_kernel,
        out_shape=near((rows, cols), F32),
        in_specs=[VM],
        out_specs=VM,
        compiler_params=ROOM,
    )(swap(partial, "rep"))
    aggregate = held(lax.all_gather(own_aggregate, "feat", axis=0, tiled=True))
    output, pay = pl.pallas_call(
        node_kernel,
        out_shape=(shape((rows, cols), F32), near((reps, rows + chunk + 8, cols), BF)),
        in_specs=[VM, VM, VM, VM],
        out_specs=(VM, VM),
        compiler_params=ROOM,
    )(aggregate, cotangents, near_weight, near_bias)
    sends = pl.pallas_call(
        backward_kernel,
        out_shape=near((x_count, z_count * rows + 2 * chunk + 8, cols), BF),
        in_specs=[SM, SM, VM, VM, VM],
        out_specs=VM,
        compiler_params=ROOM,
        scratch_shapes=[
            pltpu.VMEM((n_row, cols, rows), F32),
            pltpu.VMEM((dests * 2 * half, cols, rows), F32),
        ],
    )(counts, sources, own, peer, swap(pay, "rep"))
    onward = pl.pallas_call(
        middle_kernel,
        out_shape=near((z_count, rows + chunk + 8, cols), BF),
        in_specs=[VM],
        out_specs=VM,
        compiler_params=ROOM,
    )(swap(sends, "x"))
    grad_features, grad_bias, pieces = pl.pallas_call(
        finish_kernel,
        out_shape=(shape((rows, cols), F32), shape((1, cols), F32), near((reps, chunk, cols), F32)),
        in_specs=[VM],
        out_specs=(VM, VM, VM),
        compiler_params=ROOM,
    )(swap(onward, "z"))
    grad_weight = lax.all_to_all(pieces, "rep", 0, 0, tiled=True).reshape(width, cols)
    return output, grad_features, grad_weight, grad_bias[0]


def solution(mesh):
    n_row, n_rep, n_feat = mesh.devices.shape
    x_count = 4 if n_row > 4 else 2
    fine = Mesh(mesh.devices.reshape(n_row // x_count, x_count, n_rep, n_feat), ("z", "x", "rep", "feat"))
    nodes = P(("z", "x", "rep"), "feat")
    in_specs = (
        nodes,
        P(),
        P(),
        nodes,
        P(("z", "x"), "rep", None, "feat", None, None),
        P(("z", "x"), "rep", None, "feat"),
        P(("z", "x"), "rep", None),
    )
    out_specs = (nodes, nodes, P(None, "feat"), P("feat"))
    return jax.shard_map(local, mesh=fine, in_specs=in_specs, out_specs=out_specs, check_vma=False)
```
